32 devices in a mesh: expert: 16 (over z, y, x), loop: 2 (over core).
Axes of the slice: x: 2, y: 2, z: 4, core: 2. Of those that a mesh axis runs over, the one named last changes fastest.
Arguments:
- tokens: bfloat16 [2048, 7168], P('expert', 'loop'), may hold values from -6 to 6
- expert_ids: int32 [2048, 8], P('expert'), may hold values from 0 to 255, all different within a row; in each aligned block of 128 rows (0 to 127, 128 to 255, ...) at most 8 rows name the same one
- route_weights: float32 [2048, 8], P('expert'), may hold values from 0.1 to 1
- up_proj: bfloat16 [16, 7168, 1024], P('expert', None, 'loop'), may hold values from -0.0625 to 0.0625
- down_proj: bfloat16 [16, 1024, 7168], P('expert', None, 'loop'), may hold values from -0.1875 to 0.1875
Outputs:
- combined: bfloat16 [2048, 7168], P('expert', 'loop')
The draws below stay inside these ranges and needn't reach their ends.
Inputs may be any that keep to these rules, and one draw needn't show every extreme that they name: `expert_ids`: each row names 8 different experts. Among the 128 rows held by one device along `expert`, no expert is chosen by more than 8 rows, a bound that some block reaches.
All inputs are finite; a program needn't handle non-finite values.
Results may differ from the reference program's by a relative error of at most 0.0058.
Values may be sent and summed in bfloat16 or wider, within the bound.
No kernel may reach another device: no remote copies, remote signals or barrier semaphores. Data moves between devices by JAX's collectives and lax.ppermute only.
A program may use at most 64 MiB of HBM per device.

```python
import math
import jax
import jax.numpy as jnp
import numpy as np
from jax import lax

D = 7168
FF = 1024
EXPERTS = 256
TOPK = 8
TOK_GRP = 128
CAP = 8
FLIGHT = 16
TOKENS = 2048
N_EXPERT = 16


def block_scale(own_key, shape, shards, low, high):
    loudness = 1.0
    for dim, shards_of in shards:
        steps = jax.random.uniform(jax.random.fold_in(jax.random.fold_in(own_key, 6), dim), (shards_of,), jnp.float32, low / len(shards), high / len(shards))
        loudness = loudness * jnp.repeat(jnp.exp(steps), shape[dim] // shards_of).reshape((-1,) + (1,) * (len(shape) - 1 - dim))
    return loudness


def shared_out(key, own, number, rows, amount, top, most, slope):
    order = jax.random.permutation(key, amount)
    crowded, usual = load_shares(amount, rows * top, most, slope, True), load_shares(amount, rows * top, most, slope, False)
    places = jnp.arange(amount)

    def named(sizes, rotation):
        used = int((sizes > 0).sum())
        fixed = max(1, used // 4)
        moved = fixed + (places - fixed + rotation * (used - fixed)) % max(1, amount - fixed)
        return jnp.zeros((amount,), jnp.int32).at[order[jnp.where(places < fixed, places, moved)]].set(jnp.asarray(sizes, jnp.int32))

    sizes = jnp.where(number % 4 == 0, named(crowded, number // 4), named(usual, number - number // 4 - 1))
    mixed = jax.random.permutation(jax.random.fold_in(own, 3), amount)
    source_of, taker = mixed[0:amount // 2 * 2:2], mixed[1:amount // 2 * 2:2]
    room = jnp.minimum(sizes[source_of] - 1, most - sizes[taker]) // 2
    room = jnp.where((source_of == order[0]) | (taker == order[0]) | (sizes[taker] == 0), 0, jnp.maximum(room, 0))
    moved = jax.random.randint(jax.random.fold_in(own, 4), (amount // 2,), 0, 1 << 20) % (room + 1)
    sizes = sizes.at[source_of].add(-moved).at[taker].add(moved)
    items = jnp.searchsorted(jnp.cumsum(sizes), jnp.arange(rows * top), side="right").astype(jnp.int32)
    grid = items.reshape(top, rows).T
    grid = grid[jax.random.permutation(jax.random.fold_in(own, 1), rows)]
    rotation = jax.random.randint(jax.random.fold_in(own, 2), (rows, 1), 0, top)
    return jnp.take_along_axis(grid, (jnp.arange(top)[None, :] + rotation) % top, axis=1)


def load_shares(amount, total, reach, slope, full):
    weights = [(1 << 20) // math.isqrt(standing ** slope) + 1 for standing in range(1, amount + 1)]
    largest = reach if full else min(reach, max(-(-total // amount), total * weights[0] // sum(weights)))
    least = 1 if total - largest >= amount - 1 else 0
    given, surplus = [largest] + [least] * (amount - 1), total - largest - least * (amount - 1)
    while surplus > 0:
        movable = [i for i in range(1, amount) if given[i] < largest] or [i for i in range(1, amount) if given[i] < reach]
        whole, remaining = sum([weights[i] for i in movable]), surplus
        for i in movable:
            extra = min(reach - given[i], max(1, remaining * weights[i] // whole), surplus)
            given[i] = given[i] + extra
            surplus = surplus - extra
    return np.array(given)


def gaussian(key, extent, deviation, bound, pieces=(), held_as=jnp.bfloat16):
    level = block_scale(key, extent, pieces, -0.22, 0.18) if pieces else 1.0
    array = jax.random.normal(key, extent, jnp.float32) * deviation * level
    return jnp.minimum(jnp.maximum(array, -bound), bound).astype(held_as)


def setup_inputs(seed: int = 0) -> dict:
    splits = jax.random.split(jax.random.key(seed), 6)
    tokens = gaussian(splits[0], (TOKENS, D), 1.0, 6.0, ((0, 16), (1, 2)))
    expert_ids_keys = jax.random.split(jax.random.fold_in(splits[1], 1), TOKENS // TOK_GRP)
    expert_ids_turns = jax.random.permutation(jax.random.fold_in(splits[1], 3), TOKENS // TOK_GRP)
    expert_ids = jax.vmap(lambda own, number: shared_out(jax.random.fold_in(splits[1], 2), own, number, TOK_GRP, EXPERTS, TOPK, CAP, 2))(expert_ids_keys, expert_ids_turns).reshape((TOKENS, TOPK))
    route_weights = jnp.clip(0.1 + 0.9 * jax.random.uniform(splits[2], (TOKENS, TOPK), jnp.float32) ** block_scale(splits[2], (TOKENS, TOPK), ((0, 16),), -0.2, 0.2), 0.1, 1.0)
    up_proj = gaussian(splits[3], (FLIGHT, D, FF), D ** -0.5, 0.0625, ((0, 16), (2, 2)))
    down_proj = gaussian(splits[4], (FLIGHT, FF, D), FF ** -0.5, 0.1875, ((0, 16), (2, 2)))
    return {"tokens": tokens, "expert_ids": expert_ids, "route_weights": route_weights, "up_proj": up_proj, "down_proj": down_proj}


def reference(tokens, expert_ids, route_weights, up_proj, down_proj):
    flight = up_proj.shape[0]
    slots = N_EXPERT * CAP
    zero_acc = jnp.zeros((tokens.shape[0], tokens.shape[1]), jnp.float32)

    def one_expert(summed, members):
        expert_id, up_block, down_block = members
        matches = expert_ids == expert_id
        weight = jnp.sum(jnp.where(matches, route_weights, jnp.zeros_like(route_weights)), axis=1)
        chosen = jnp.any(matches, axis=1)
        positions = jnp.nonzero(chosen, size=slots, fill_value=0)[0].astype(jnp.int32)
        in_use = jnp.arange(slots, dtype=jnp.int32) < jnp.sum(chosen.astype(jnp.int32))
        gathered = tokens[positions].astype(jnp.float32)
        up_sums = jnp.dot(gathered, up_block.astype(jnp.float32))
        hidden = jax.nn.silu(up_sums).astype(jnp.bfloat16)
        out_rows = jnp.dot(hidden.astype(jnp.float32), down_block.astype(jnp.float32)).astype(jnp.bfloat16)
        slot_weight = jnp.where(in_use, weight[positions], jnp.zeros_like(weight[positions]))
        scaled = slot_weight[:, None] * out_rows.astype(jnp.float32)
        return summed.at[positions].add(scaled), None

    numbers = jnp.arange(flight, dtype=jnp.int32)
    summed, _ = lax.scan(one_expert, zero_acc, (numbers, up_proj, down_proj))
    return summed.astype(jnp.bfloat16)
```

```python
import jax
import jax.numpy as jnp
from jax import lax
from jax.experimental import pallas as pl
from jax.experimental.pallas import tpu as pltpu
from jax.sharding import PartitionSpec as P

BF16, F32 = jnp.bfloat16, jnp.float32


def slot_onehot(ids, flight, capacity):
    top, tok = ids.shape
    experts = lax.broadcasted_iota(jnp.int32, (flight, tok), 0)
    chosen = jnp.zeros((flight, tok), F32)
    for k in range(top):
        chosen = jnp.where(ids[k : k + 1, :] == experts, 1.0, chosen)
    before = lax.broadcasted_iota(jnp.int32, (tok, tok), 0) < lax.broadcasted_iota(
        jnp.int32, (tok, tok), 1
    )
    rank = jnp.dot(
        chosen.astype(BF16), before.astype(F32).astype(BF16), preferred_element_type=F32
    )
    rank = jnp.where(chosen > 0.5, rank, -1.0)
    places = lax.broadcasted_iota(jnp.int32, (flight, capacity, tok), 1).astype(F32)
    return rank[:, None, :] == places


def dispatch_kernel(flight, capacity, ids_ref, tokens_ref, out_ref):
    tok = ids_ref.shape[1]
    picked = slot_onehot(ids_ref[...], flight, capacity)
    onehot = jnp.where(picked, 1.0, 0.0).reshape(flight * capacity, tok).astype(BF16)
    out_ref[...] = jnp.dot(onehot, tokens_ref[...], preferred_element_type=F32).astype(BF16)


def combine_kernel(flight, capacity, ids_ref, weights_ref, rows_ref, out_ref):
    ids = ids_ref[...]
    top, tok = ids.shape
    picked = slot_onehot(ids, flight, capacity)
    experts = lax.broadcasted_iota(jnp.int32, (flight, tok), 0)
    weight = jnp.zeros((flight, tok), F32)
    for k in range(top):
        weight = jnp.where(ids[k : k + 1, :] == experts, weights_ref[k : k + 1, :], weight)
    mix = jnp.where(picked, weight[:, None, :], 0.0).reshape(flight * capacity, tok)
    total = None
    for _ in range(3):
        part = mix.astype(BF16)
        mix = mix - part.astype(F32)
        term = lax.dot_general(
            part, rows_ref[...], (((0,), (0,)), ((), ())), preferred_element_type=F32
        )
        total = term if total is None else total + term
    out_ref[...] = total.astype(BF16)


def matmul_kernel(finish, half_ref, x_ref, w_ref, *refs):
    out_ref, acc = refs[-2], refs[-1]
    step = pl.program_id(0)
    term = jnp.dot(x_ref[...], w_ref[0], preferred_element_type=F32)

    @pl.when(step == 0)
    def _():
        acc[...] = term if len(refs) == 2 else refs[0][...] + term

    @pl.when(step > 0)
    def _():
        acc[...] += term

    @pl.when(step == pl.num_programs(0) - 1)
    def _():
        out_ref[...] = finish(acc[...]).astype(out_ref.dtype)


def matmul_rows(half, x, w, start, finish, dtype, block):
    rows, depth = x.shape
    width = w.shape[2]
    steps = depth // block
    whole = pl.BlockSpec((rows, width), lambda k, h: (0, 0))
    return pl.pallas_call(
        lambda *refs: matmul_kernel(finish, *refs),
        grid_spec=pltpu.PrefetchScalarGridSpec(
            num_scalar_prefetch=1,
            grid=(steps,),
            in_specs=[
                pl.BlockSpec((rows, block), lambda k, h: (0, k)),
                pl.BlockSpec((1, block, width), lambda k, h: (0, h[0] * steps + k, 0)),
            ]
            + ([] if start is None else [whole]),
            out_specs=whole,
            scratch_shapes=[pltpu.VMEM((rows, width), F32)],
        ),
        out_shape=jax.ShapeDtypeStruct((rows, width), dtype),
        compiler_params=pltpu.CompilerParams(vmem_limit_bytes=48 * 2**20),
    )(half, x, w, *([] if start is None else [start]))


def silu(v):
    return v / (1.0 + jnp.exp(-v))


def same(v):
    return v


def on_device(tokens, expert_ids, route_weights, up_proj, down_proj):
    tok_rows, width = tokens.shape
    capacity = tok_rows // 16
    owners = lax.axis_size("expert")
    loops = lax.axis_size("loop")
    per_owner = up_proj.shape[0]
    flight = owners * per_owner
    slots = flight * capacity
    ids_t, weights_t = expert_ids.T, route_weights.T

    outgoing = pl.pallas_call(
        lambda *refs: dispatch_kernel(flight, capacity, *refs),
        out_shape=jax.ShapeDtypeStruct((slots, width), BF16),
    )(ids_t, tokens)
    arrived = lax.all_to_all(
        outgoing.reshape(owners, per_owner * capacity, width),
        "expert",
        split_axis=0,
        concat_axis=0,
        tiled=True,
    ).reshape(slots, width)

    me = lax.axis_index("loop").astype(jnp.int32).reshape(1)
    if loops == 2:
        swap = [(0, 1), (1, 0)]
        other = lax.ppermute(arrived, "loop", swap)
        up_block = width // 7
        part = matmul_rows(me, arrived, up_proj, None, same, F32, up_block)
        hidden = matmul_rows(1 - me, other, up_proj, part, silu, BF16, up_block)
        hidden_other = lax.ppermute(hidden, "loop", swap)
        part = matmul_rows(me, hidden, down_proj, None, same, F32, hidden.shape[1] // 4)
        out_rows = matmul_rows(
            1 - me, hidden_other, down_proj, part, same, BF16, hidden.shape[1] // 4
        )
    else:
        full = lax.all_gather(arrived, "loop", axis=1, tiled=True)
        zero = jnp.zeros_like(me)
        hidden = matmul_rows(zero, full, up_proj, None, silu, BF16, full.shape[1] // 7)
        hidden_full = lax.all_gather(hidden, "loop", axis=1, tiled=True)
        out_rows = matmul_rows(zero, hidden_full, down_proj, None, same, BF16, hidden_full.shape[1] // 8)

    returned = lax.all_to_all(
        out_rows.reshape(owners, per_owner * capacity, width),
        "expert",
        split_axis=0,
        concat_axis=0,
        tiled=True,
    ).reshape(slots, width)
    return pl.pallas_call(
        lambda *refs: combine_kernel(flight, capacity, *refs),
        out_shape=jax.ShapeDtypeStruct((tok_rows, width), BF16),
    )(ids_t, weights_t, returned)


def solution(mesh):
    return jax.shard_map(
        on_device,
        mesh=mesh,
        in_specs=(
            P("expert", "loop"),
            P("expert", None),
            P("expert", None),
            P("expert", None, "loop"),
            P("expert", None, "loop"),
        ),
        out_specs=P("expert", "loop"),
        check_vma=False,
    )
```

```python
import jax
import jax.numpy as jnp
from jax import lax
from jax.experimental import pallas as pl
from jax.experimental.pallas import tpu as pltpu
from jax.sharding import PartitionSpec as P

BF16, F32 = jnp.bfloat16, jnp.float32


def slot_onehot(ids, flight, capacity):
    top, tok = ids.shape
    experts = lax.broadcasted_iota(jnp.int32, (flight, tok), 0)
    chosen = jnp.zeros((flight, tok), F32)
    for k in range(top):
        chosen = jnp.where(ids[k : k + 1, :] == experts, 1.0, chosen)
    before = lax.broadcasted_iota(jnp.int32, (tok, tok), 0) < lax.broadcasted_iota(
        jnp.int32, (tok, tok), 1
    )
    rank = jnp.dot(
        chosen.astype(BF16), before.astype(F32).astype(BF16), preferred_element_type=F32
    )
    rank = jnp.where(chosen > 0.5, rank, -1.0)
    places = lax.broadcasted_iota(jnp.int32, (flight, capacity, tok), 1).astype(F32)
    return rank[:, None, :] == places


def dispatch_kernel(flight, capacity, ids_ref, tokens_ref, out_ref):
    tok = ids_ref.shape[1]
    picked = slot_onehot(ids_ref[...], flight, capacity)
    onehot = jnp.where(picked, 1.0, 0.0).reshape(flight * capacity, tok).astype(BF16)
    out_ref[...] = jnp.dot(onehot, tokens_ref[...], preferred_element_type=F32).astype(BF16)


def combine_kernel(flight, capacity, ids_ref, weights_ref, rows_ref, out_ref):
    ids = ids_ref[...]
    top, tok = ids.shape
    picked = slot_onehot(ids, flight, capacity)
    experts = lax.broadcasted_iota(jnp.int32, (flight, tok), 0)
    weight = jnp.zeros((flight, tok), F32)
    for k in range(top):
        weight = jnp.where(ids[k : k + 1, :] == experts, weights_ref[k : k + 1, :], weight)
    mix = jnp.where(picked, weight[:, None, :], 0.0).reshape(flight * capacity, tok)
    total = None
    for _ in range(3):
        part = mix.astype(BF16)
        mix = mix - part.astype(F32)
        term = lax.dot_general(
            part, rows_ref[...], (((0,), (0,)), ((), ())), preferred_element_type=F32
        )
        total = term if total is None else total + term
    out_ref[...] = total.astype(BF16)


def whole_call(kernel, shape, dtype, *arrays):
    return pl.pallas_call(
        kernel,
        in_specs=[pl.BlockSpec(memory_space=pltpu.VMEM)] * len(arrays),
        out_specs=pl.BlockSpec(memory_space=pltpu.VMEM),
        out_shape=jax.ShapeDtypeStruct(shape, dtype),
        compiler_params=pltpu.CompilerParams(vmem_limit_bytes=16 * 2**20),
    )(*arrays)


def half_dot(x_ref, w_ref, core):
    depth = x_ref.shape[1]
    rows = pl.ds(pl.multiple_of(core * depth, depth), depth)
    return jnp.dot(x_ref[...], w_ref[0, rows, :], preferred_element_type=F32)


def mine_kernel(x_ref, w_ref, out_ref):
    out_ref[...] = half_dot(x_ref, w_ref, lax.axis_index("loop"))


def up_kernel(part_ref, x_ref, w_ref, out_ref):
    out_ref[...] = silu(part_ref[...] + half_dot(x_ref, w_ref, 1 - lax.axis_index("loop"))).astype(BF16)


def down_kernel(part_ref, x_ref, w_ref, out_ref):
    out_ref[...] = (part_ref[...] + half_dot(x_ref, w_ref, 1 - lax.axis_index("loop"))).astype(BF16)


def plain_up_kernel(x_ref, w_ref, out_ref):
    out_ref[...] = silu(jnp.dot(x_ref[...], w_ref[0], preferred_element_type=F32)).astype(BF16)


def plain_down_kernel(x_ref, w_ref, out_ref):
    out_ref[...] = jnp.dot(x_ref[...], w_ref[0], preferred_element_type=F32).astype(BF16)


def silu(v):
    return v / (1.0 + jnp.exp(-v))


def on_device(tokens, expert_ids, route_weights, up_proj, down_proj):
    tok_rows, width = tokens.shape
    capacity = tok_rows // 16
    owners = lax.axis_size("expert")
    loops = lax.axis_size("loop")
    per_owner = up_proj.shape[0]
    flight = owners * per_owner
    slots = flight * capacity
    ids_t, weights_t = expert_ids.T, route_weights.T

    outgoing = pl.pallas_call(
        lambda *refs: dispatch_kernel(flight, capacity, *refs),
        out_shape=jax.ShapeDtypeStruct((slots, width), BF16),
        cost_estimate=pl.CostEstimate(flops=10**11, bytes_accessed=10**8, transcendentals=0),
        compiler_params=pltpu.CompilerParams(vmem_limit_bytes=16 * 2**20),
    )(ids_t, tokens)
    arrived = lax.all_to_all(
        outgoing.reshape(owners, per_owner * capacity, width),
        "expert",
        split_axis=0,
        concat_axis=0,
        tiled=True,
    ).reshape(slots, width)

    if loops == 2:
        swap = [(0, 1), (1, 0)]
        theirs = lax.ppermute(arrived, "loop", swap)
        units = up_proj.shape[2]
        part = whole_call(mine_kernel, (slots, units), F32, arrived, up_proj)
        hidden = whole_call(up_kernel, (slots, units), BF16, part, theirs, up_proj)
        hidden_theirs = lax.ppermute(hidden, "loop", swap)
        part = whole_call(mine_kernel, (slots, width), F32, hidden, down_proj)
        out_rows = whole_call(down_kernel, (slots, width), BF16, part, hidden_theirs, down_proj)
    else:
        full = lax.all_gather(arrived, "loop", axis=1, tiled=True)
        hidden = whole_call(plain_up_kernel, (slots, up_proj.shape[2]), BF16, full, up_proj)
        hidden = lax.all_gather(hidden, "loop", axis=1, tiled=True)
        out_rows = whole_call(plain_down_kernel, (slots, width), BF16, hidden, down_proj)

    returned = lax.all_to_all(
        out_rows.reshape(owners, per_owner * capacity, width),
        "expert",
        split_axis=0,
        concat_axis=0,
        tiled=True,
    ).reshape(slots, width)
    return pl.pallas_call(
        lambda *refs: combine_kernel(flight, capacity, *refs),
        out_shape=jax.ShapeDtypeStruct((tok_rows, width), BF16),
        compiler_params=pltpu.CompilerParams(vmem_limit_bytes=16 * 2**20),
    )(ids_t, weights_t, returned)


def solution(mesh):
    return jax.shard_map(
        on_device,
        mesh=mesh,
        in_specs=(
            P("expert", "loop"),
            P("expert", None),
            P("expert", None),
            P("expert", None, "loop"),
            P("expert", None, "loop"),
        ),
        out_specs=P("expert", "loop"),
        check_vma=False,
    )
```

```python
import jax
import jax.numpy as jnp
from jax import lax
from jax.experimental import pallas as pl
from jax.experimental.pallas import tpu as pltpu
from jax.sharding import PartitionSpec as P

BF16, F32 = jnp.bfloat16, jnp.float32
COMBINE_BLOCKS, MIX_PARTS = 7, 2


def slot_tables(ids_ref, weights_ref, onehot_ref, mix_ref, flight, capacity):
    top, tok = ids_ref.shape
    experts = lax.broadcasted_iota(jnp.int32, (flight, tok), 0)
    chosen = jnp.zeros((flight, tok), F32)
    weight = jnp.zeros((flight, tok), F32)
    for k in range(top):
        names = ids_ref[k : k + 1, :] == experts
        chosen = jnp.where(names, 1.0, chosen)
        weight = jnp.where(names, weights_ref[k : k + 1, :], weight)
    before = lax.broadcasted_iota(jnp.int32, (tok, tok), 0) < lax.broadcasted_iota(
        jnp.int32, (tok, tok), 1
    )
    rank = jnp.dot(
        chosen.astype(BF16), jnp.where(before, 1.0, 0.0).astype(BF16), preferred_element_type=F32
    )
    rank = jnp.where(chosen > 0.5, rank, -1.0)
    places = lax.broadcasted_iota(jnp.int32, (flight, capacity, tok), 1).astype(F32)
    picked = rank[:, None, :] == places
    onehot_ref[...] = jnp.where(picked, 1.0, 0.0).reshape(flight * capacity, tok).astype(BF16)
    mix = jnp.where(picked, weight[:, None, :], 0.0).reshape(flight * capacity, tok).T
    for i in range(MIX_PARTS):
        part = mix.astype(BF16)
        mix_ref[i] = part
        mix = mix - part.astype(F32)


def column_blocks(width, count):
    block = width // count
    return [slice(i * block, (i + 1) * block) for i in range(count)]


def read_kernel(
    flight, capacity, ids_ref, weights_ref, tokens_ref, held, onehot_ref, mix_ref, ids, weights, sems
):
    copies = [
        pltpu.make_async_copy(ids_ref, ids, sems.at[0]),
        pltpu.make_async_copy(weights_ref, weights, sems.at[1]),
        pltpu.make_async_copy(tokens_ref, held, sems.at[2]),
    ]
    for copy in copies:
        copy.start()
    copies[0].wait()
    copies[1].wait()
    slot_tables(ids, weights, onehot_ref, mix_ref, flight, capacity)
    copies[2].wait()


def pick_kernel(onehot_ref, held_ref, out_ref):
    out_ref[...] = jnp.dot(onehot_ref[...], held_ref[...], preferred_element_type=F32).astype(BF16)


def dispatch(ids_t, weights_t, tokens, flight, capacity):
    hbm = pl.BlockSpec(memory_space=pltpu.HBM)
    vmem = pl.BlockSpec(memory_space=pltpu.VMEM)
    slots, tok = flight * capacity, tokens.shape[0]
    held, onehot, mix = pl.pallas_call(
        lambda *refs: read_kernel(flight, capacity, *refs),
        in_specs=[hbm, hbm, hbm],
        out_specs=[vmem, vmem, vmem],
        out_shape=[
            jax.ShapeDtypeStruct(tokens.shape, BF16),
            jax.ShapeDtypeStruct((slots, tok), BF16),
            jax.ShapeDtypeStruct((MIX_PARTS, tok, slots), BF16),
        ],
        scratch_shapes=[
            pltpu.VMEM(ids_t.shape, jnp.int32),
            pltpu.VMEM(weights_t.shape, F32),
            pltpu.SemaphoreType.DMA((3,)),
        ],
        cost_estimate=pl.CostEstimate(flops=0, bytes_accessed=0, transcendentals=0),
        compiler_params=pltpu.CompilerParams(vmem_limit_bytes=16 * 2**20),
    )(*(pltpu.with_memory_space_constraint(a, pltpu.HBM) for a in (ids_t, weights_t, tokens)))
    outgoing = pl.pallas_call(
        pick_kernel,
        in_specs=[vmem, vmem],
        out_specs=vmem,
        out_shape=jax.ShapeDtypeStruct((slots, tokens.shape[1]), BF16),
        cost_estimate=pl.CostEstimate(flops=10**11, bytes_accessed=10**8, transcendentals=0),
        compiler_params=pltpu.CompilerParams(vmem_limit_bytes=16 * 2**20),
    )(onehot, held)
    return outgoing, mix


def combine_kernel(mix_ref, rows_ref, out_ref, held, sems):
    copies = []
    for i, at in enumerate(column_blocks(held.shape[1], COMBINE_BLOCKS)):
        rows = rows_ref[:, at]
        held[:, at] = sum(
            jnp.dot(mix_ref[k], rows, preferred_element_type=F32) for k in range(MIX_PARTS)
        ).astype(BF16)
        copies.append(pltpu.make_async_copy(held.at[:, at], out_ref.at[:, at], sems.at[i]))
        copies[-1].start()
    for copy in copies:
        copy.wait()


def combine(mix, rows):
    tok, width = mix.shape[1], rows.shape[1]
    vmem = pl.BlockSpec(memory_space=pltpu.VMEM)
    return pl.pallas_call(
        combine_kernel,
        in_specs=[vmem, vmem],
        out_specs=pl.BlockSpec(memory_space=pltpu.HBM),
        out_shape=jax.ShapeDtypeStruct((tok, width), BF16),
        scratch_shapes=[
            pltpu.VMEM((tok, width), BF16),
            pltpu.SemaphoreType.DMA((COMBINE_BLOCKS,)),
        ],
        compiler_params=pltpu.CompilerParams(vmem_limit_bytes=16 * 2**20),
    )(mix, rows)


def whole_call(kernel, out, *arrays):
    return pl.pallas_call(
        kernel,
        in_specs=[pl.BlockSpec(memory_space=pltpu.VMEM)] * len(arrays),
        out_specs=jax.tree.map(lambda _: pl.BlockSpec(memory_space=pltpu.VMEM), out),
        out_shape=out,
        cost_estimate=pl.CostEstimate(flops=2**29, bytes_accessed=0, transcendentals=0),
        compiler_params=pltpu.CompilerParams(vmem_limit_bytes=16 * 2**20),
    )(*arrays)


def half_dot(x_ref, w_ref, core):
    depth = x_ref.shape[1]
    rows = pl.ds(pl.multiple_of(core * depth, depth), depth)
    return jnp.dot(x_ref[...], w_ref[0, rows, :], preferred_element_type=F32)


def mine_kernel(x_ref, w_ref, out_ref):
    out_ref[...] = half_dot(x_ref, w_ref, lax.axis_index("loop"))


def up_kernel(part_ref, x_ref, w_ref, out_ref):
    out_ref[...] = silu(part_ref[...] + half_dot(x_ref, w_ref, 1 - lax.axis_index("loop"))).astype(BF16)


def down_kernel(part_ref, x_ref, w_ref, out_ref):
    out_ref[...] = (part_ref[...] + half_dot(x_ref, w_ref, 1 - lax.axis_index("loop"))).astype(BF16)


def plain_up_kernel(x_ref, w_ref, out_ref):
    out_ref[...] = silu(jnp.dot(x_ref[...], w_ref[0], preferred_element_type=F32)).astype(BF16)


def plain_down_kernel(x_ref, w_ref, out_ref):
    out_ref[...] = jnp.dot(x_ref[...], w_ref[0], preferred_element_type=F32).astype(BF16)


def silu(v):
    return v / (1.0 + jnp.exp(-v))


def on_device(tokens, expert_ids, route_weights, up_proj, down_proj):
    tok_rows, width = tokens.shape
    capacity = tok_rows // 16
    owners = lax.axis_size("expert")
    loops = lax.axis_size("loop")
    per_owner = up_proj.shape[0]
    flight = owners * per_owner
    slots = flight * capacity
    ids_t, weights_t = expert_ids.T, route_weights.T

    outgoing, mix = dispatch(ids_t, weights_t, tokens, flight, capacity)
    arrived = lax.all_to_all(
        outgoing.reshape(owners, per_owner * capacity, width),
        "expert",
        split_axis=0,
        concat_axis=0,
        tiled=True,
    ).reshape(slots, width)

    if loops == 2:
        swap = [(0, 1), (1, 0)]
        theirs = lax.ppermute(arrived, "loop", swap)
        units = up_proj.shape[2]
        part = whole_call(mine_kernel, jax.ShapeDtypeStruct((slots, units), F32), arrived, up_proj)
        hidden = whole_call(up_kernel, jax.ShapeDtypeStruct((slots, units), BF16), part, theirs, up_proj)
        hidden_theirs = lax.ppermute(hidden, "loop", swap)
        part = whole_call(mine_kernel, jax.ShapeDtypeStruct((slots, width), F32), hidden, down_proj)
        out_rows = whole_call(down_kernel, jax.ShapeDtypeStruct((slots, width), BF16), part, hidden_theirs, down_proj)
    else:
        full = lax.all_gather(arrived, "loop", axis=1, tiled=True)
        hidden = whole_call(plain_up_kernel, jax.ShapeDtypeStruct((slots, up_proj.shape[2]), BF16), full, up_proj)
        hidden = lax.all_gather(hidden, "loop", axis=1, tiled=True)
        out_rows = whole_call(plain_down_kernel, jax.ShapeDtypeStruct((slots, width), BF16), hidden, down_proj)

    returned = lax.all_to_all(
        out_rows.reshape(owners, per_owner * capacity, width),
        "expert",
        split_axis=0,
        concat_axis=0,
        tiled=True,
    ).reshape(slots, width)
    return combine(mix, returned)


def solution(mesh):
    return jax.shard_map(
        on_device,
        mesh=mesh,
        in_specs=(
            P("expert", "loop"),
            P("expert", None),
            P("expert", None),
            P("expert", None, "loop"),
            P("expert", None, "loop"),
        ),
        out_specs=P("expert", "loop"),
        check_vma=False,
    )
```

```python
import jax
import jax.numpy as jnp
from jax import lax
from jax.experimental import pallas as pl
from jax.experimental.pallas import tpu as pltpu
from jax.sharding import PartitionSpec as P

BF16, F32 = jnp.bfloat16, jnp.float32
COMBINE_BLOCKS, MIX_PARTS = 7, 2


def slot_tables(ids_ref, weights_ref, onehot_ref, mix_ref, flight, capacity):
    top, tok = ids_ref.shape
    experts = lax.broadcasted_iota(jnp.int32, (flight, tok), 0)
    chosen = jnp.zeros((flight, tok), F32)
    weight = jnp.zeros((flight, tok), F32)
    for k in range(top):
        names = ids_ref[k : k + 1, :] == experts
        chosen = jnp.where(names, 1.0, chosen)
        weight = jnp.where(names, weights_ref[k : k + 1, :], weight)
    before = lax.broadcasted_iota(jnp.int32, (tok, tok), 0) < lax.broadcasted_iota(
        jnp.int32, (tok, tok), 1
    )
    rank = jnp.dot(
        chosen.astype(BF16), jnp.where(before, 1.0, 0.0).astype(BF16), preferred_element_type=F32
    )
    rank = jnp.where(chosen > 0.5, rank, -1.0)
    places = lax.broadcasted_iota(jnp.int32, (flight, capacity, tok), 1).astype(F32)
    picked = rank[:, None, :] == places
    onehot_ref[...] = jnp.where(picked, 1.0, 0.0).reshape(flight * capacity, tok).astype(BF16)
    mix = jnp.where(picked, weight[:, None, :], 0.0).reshape(flight * capacity, tok).T
    for i in range(MIX_PARTS):
        part = mix.astype(BF16)
        mix_ref[i] = part
        mix = mix - part.astype(F32)


def column_blocks(width, count):
    block = width // count
    return [slice(i * block, (i + 1) * block) for i in range(count)]


def read_kernel(
    flight, capacity, ids_ref, weights_ref, tokens_ref, held, onehot_ref, mix_ref, ids, weights, sems
):
    copies = [
        pltpu.make_async_copy(ids_ref, ids, sems.at[0]),
        pltpu.make_async_copy(weights_ref, weights, sems.at[1]),
        pltpu.make_async_copy(tokens_ref, held, sems.at[2]),
    ]
    for copy in copies:
        copy.start()
    copies[0].wait()
    copies[1].wait()
    slot_tables(ids, weights, onehot_ref, mix_ref, flight, capacity)
    copies[2].wait()


def pick_kernel(onehot_ref, held_ref, out_ref):
    owners, cores, rows, block = out_ref.shape
    for core in range(cores):
        part = held_ref[:, core * block : (core + 1) * block]
        picked = jnp.dot(onehot_ref[...], part, preferred_element_type=F32).astype(BF16)
        out_ref[:, core] = picked.reshape(owners, rows, block)


def dispatch(ids_t, weights_t, tokens, flight, capacity, shape):
    hbm = pl.BlockSpec(memory_space=pltpu.HBM)
    vmem = pl.BlockSpec(memory_space=pltpu.VMEM)
    slots, tok = flight * capacity, tokens.shape[0]
    held, onehot, mix = pl.pallas_call(
        lambda *refs: read_kernel(flight, capacity, *refs),
        in_specs=[hbm, hbm, hbm],
        out_specs=[vmem, vmem, vmem],
        out_shape=[
            jax.ShapeDtypeStruct(tokens.shape, BF16),
            jax.ShapeDtypeStruct((slots, tok), BF16),
            jax.ShapeDtypeStruct((MIX_PARTS, tok, slots), BF16),
        ],
        scratch_shapes=[
            pltpu.VMEM(ids_t.shape, jnp.int32),
            pltpu.VMEM(weights_t.shape, F32),
            pltpu.SemaphoreType.DMA((3,)),
        ],
        cost_estimate=pl.CostEstimate(flops=0, bytes_accessed=0, transcendentals=0),
        compiler_params=pltpu.CompilerParams(vmem_limit_bytes=16 * 2**20),
    )(*(pltpu.with_memory_space_constraint(a, pltpu.HBM) for a in (ids_t, weights_t, tokens)))
    outgoing = pl.pallas_call(
        pick_kernel,
        in_specs=[vmem, vmem],
        out_specs=vmem,
        out_shape=jax.ShapeDtypeStruct(shape, BF16),
        cost_estimate=pl.CostEstimate(flops=10**11, bytes_accessed=10**8, transcendentals=0),
        compiler_params=pltpu.CompilerParams(vmem_limit_bytes=16 * 2**20),
    )(onehot, held)
    return outgoing, mix


def combine_kernel(mix_ref, rows_ref, out_ref, held, sems):
    copies = []
    for i, at in enumerate(column_blocks(held.shape[1], COMBINE_BLOCKS)):
        rows = rows_ref[:, at]
        held[:, at] = sum(
            jnp.dot(mix_ref[k], rows, preferred_element_type=F32) for k in range(MIX_PARTS)
        ).astype(BF16)
        copies.append(pltpu.make_async_copy(held.at[:, at], out_ref.at[:, at], sems.at[i]))
        copies[-1].start()
    for copy in copies:
        copy.wait()


def combine(mix, rows):
    tok, width = mix.shape[1], rows.shape[1]
    vmem = pl.BlockSpec(memory_space=pltpu.VMEM)
    return pl.pallas_call(
        combine_kernel,
        in_specs=[vmem, vmem],
        out_specs=pl.BlockSpec(memory_space=pltpu.HBM),
        out_shape=jax.ShapeDtypeStruct((tok, width), BF16),
        scratch_shapes=[
            pltpu.VMEM((tok, width), BF16),
            pltpu.SemaphoreType.DMA((COMBINE_BLOCKS,)),
        ],
        compiler_params=pltpu.CompilerParams(vmem_limit_bytes=16 * 2**20),
    )(mix, rows)


def whole_call(kernel, out, *arrays):
    return pl.pallas_call(
        kernel,
        in_specs=[pl.BlockSpec(memory_space=pltpu.VMEM)] * len(arrays),
        out_specs=jax.tree.map(lambda _: pl.BlockSpec(memory_space=pltpu.VMEM), out),
        out_shape=out,
        cost_estimate=pl.CostEstimate(flops=2**29, bytes_accessed=0, transcendentals=0),
        compiler_params=pltpu.CompilerParams(vmem_limit_bytes=16 * 2**20),
    )(*arrays)


def up_kernel(x_ref, w_ref, out_ref):
    owners, cores, rows, block = x_ref.shape
    me = lax.axis_index("loop")
    total = None
    for source in range(cores):
        x = x_ref[:, source].reshape(owners * rows, block)
        at = pl.ds(pl.multiple_of((source * cores + me) * block, block), block)
        term = jnp.dot(x, w_ref[0, at, :], preferred_element_type=F32)
        total = term if total is None else total + term
    out_ref[...] = total


def up_first_kernel(x_ref, w_ref, up_ref, down_ref, out_ref):
    up_kernel(x_ref, w_ref, out_ref)


def down_dot(part_ref, other_ref, w_ref, core):
    units = part_ref.shape[1]
    hidden = silu(part_ref[...] + other_ref[...]).astype(BF16)
    at = pl.ds(pl.multiple_of(core * units, units), units)
    return jnp.dot(hidden, w_ref[0, at, :], preferred_element_type=F32)


def down_mine_kernel(part_ref, other_ref, w_ref, out_ref):
    out_ref[...] = down_dot(part_ref, other_ref, w_ref, lax.axis_index("loop"))


def down_theirs_kernel(half_ref, part_ref, other_ref, w_ref, out_ref):
    rest = down_dot(part_ref, other_ref, w_ref, 1 - lax.axis_index("loop"))
    out_ref[...] = (half_ref[...] + rest).astype(BF16)


def plain_up_kernel(x_ref, w_ref, out_ref):
    out_ref[...] = silu(jnp.dot(x_ref[...], w_ref[0], preferred_element_type=F32)).astype(BF16)


def plain_down_kernel(x_ref, w_ref, out_ref):
    out_ref[...] = jnp.dot(x_ref[...], w_ref[0], preferred_element_type=F32).astype(BF16)


def silu(v):
    return v / (1.0 + jnp.exp(-v))


def on_device(tokens, expert_ids, route_weights, up_proj, down_proj):
    tok_rows, width = tokens.shape
    capacity = tok_rows // 16
    owners = lax.axis_size("expert")
    loops = lax.axis_size("loop")
    per_owner = up_proj.shape[0]
    flight = owners * per_owner
    slots = flight * capacity
    ids_t, weights_t = expert_ids.T, route_weights.T

    if loops == 2:
        block = width // 2
        swap = [(0, 1), (1, 0)]
        up_theirs = lax.ppermute(up_proj, "loop", swap)
        outgoing, mix = dispatch(
            ids_t, weights_t, tokens, flight, capacity, (owners, 2, per_owner * capacity, block)
        )
        arrived = lax.all_to_all(
            outgoing.reshape(owners * 2, per_owner * capacity, block),
            ("expert", "loop"),
            split_axis=0,
            concat_axis=0,
            tiled=True,
        ).reshape(outgoing.shape)
        units = up_proj.shape[2]
        sums = jax.ShapeDtypeStruct((slots, units), F32)
        part_theirs = whole_call(up_first_kernel, sums, arrived, up_theirs, up_proj, down_proj)
        for_mine = lax.ppermute(part_theirs, "loop", swap)
        part_mine = whole_call(up_kernel, sums, arrived, up_proj)
        for_theirs = lax.ppermute(part_mine, "loop", swap)
        half = whole_call(
            down_mine_kernel, jax.ShapeDtypeStruct((slots, width), F32), part_mine, for_mine, down_proj
        )
        out_rows = whole_call(
            down_theirs_kernel,
            jax.ShapeDtypeStruct((slots, width), BF16),
            half,
            part_theirs,
            for_theirs,
            down_proj,
        )
    else:
        outgoing, mix = dispatch(
            ids_t, weights_t, tokens, flight, capacity, (owners, 1, per_owner * capacity, width)
        )
        arrived = lax.all_to_all(
            outgoing.reshape(owners, per_owner * capacity, width),
            "expert",
            split_axis=0,
            concat_axis=0,
            tiled=True,
        ).reshape(slots, width)
        full = lax.all_gather(arrived, "loop", axis=1, tiled=True)
        hidden = whole_call(
            plain_up_kernel, jax.ShapeDtypeStruct((slots, up_proj.shape[2]), BF16), full, up_proj
        )
        hidden = lax.all_gather(hidden, "loop", axis=1, tiled=True)
        out_rows = whole_call(
            plain_down_kernel, jax.ShapeDtypeStruct((slots, width), BF16), hidden, down_proj
        )

    returned = lax.all_to_all(
        out_rows.reshape(owners, per_owner * capacity, width),
        "expert",
        split_axis=0,
        concat_axis=0,
        tiled=True,
    ).reshape(slots, width)
    return combine(mix, returned)


def solution(mesh):
    return jax.shard_map(
        on_device,
        mesh=mesh,
        in_specs=(
            P("expert", "loop"),
            P("expert", None),
            P("expert", None),
            P("expert", None, "loop"),
            P("expert", None, "loop"),
        ),
        out_specs=P("expert", "loop"),
        check_vma=False,
    )
```

```python
import jax
import jax.numpy as jnp
from jax import lax
from jax.experimental import pallas as pl
from jax.experimental.pallas import tpu as pltpu
from jax.sharding import PartitionSpec as P

BF16, F32 = jnp.bfloat16, jnp.float32
COMBINE_BLOCKS, MIX_PARTS = 7, 2
DISPATCH_ORDER = [11, 15, 9, 13, 3, 7, 1, 5, 10, 14, 8, 12, 2, 6, 0, 4]
RETURN_ORDER = [11, 3, 10, 2, 9, 1, 8, 0, 15, 7, 14, 6, 13, 5, 12, 4]


def reorder(rows, order, size):
    return jnp.concatenate([rows[i * size : (i + 1) * size] for i in order], axis=0)


def slot_tables(ids_ref, weights_ref, onehot_ref, mix_ref, flight, capacity, orders):
    top, tok = ids_ref.shape
    experts = lax.broadcasted_iota(jnp.int32, (flight, tok), 0)
    chosen = jnp.zeros((flight, tok), F32)
    weight = jnp.zeros((flight, tok), F32)
    for k in range(top):
        names = ids_ref[k : k + 1, :] == experts
        chosen = jnp.where(names, 1.0, chosen)
        weight = jnp.where(names, weights_ref[k : k + 1, :], weight)
    before = lax.broadcasted_iota(jnp.int32, (tok, tok), 0) < lax.broadcasted_iota(
        jnp.int32, (tok, tok), 1
    )
    rank = jnp.dot(
        chosen.astype(BF16), jnp.where(before, 1.0, 0.0).astype(BF16), preferred_element_type=F32
    )
    rank = jnp.where(chosen > 0.5, rank, -1.0)
    places = lax.broadcasted_iota(jnp.int32, (flight, capacity, tok), 1).astype(F32)
    picked = rank[:, None, :] == places
    onehot = jnp.where(picked, 1.0, 0.0).reshape(flight * capacity, tok)
    mix = jnp.where(picked, weight[:, None, :], 0.0).reshape(flight * capacity, tok)
    if orders is not None:
        onehot = reorder(onehot, orders[0], capacity)
        mix = reorder(mix, orders[1], capacity)
    onehot_ref[...] = onehot.astype(BF16)
    mix = mix.T
    slots = flight * capacity
    for i in range(MIX_PARTS):
        part = mix.astype(BF16)
        mix_ref[:, i * slots : (i + 1) * slots] = part
        mix = mix - part.astype(F32)


def column_blocks(width, count):
    block = width // count
    return [slice(i * block, (i + 1) * block) for i in range(count)]


def read_kernel(
    flight, capacity, orders, ids_ref, weights_ref, tokens_ref, held, onehot_ref, mix_ref, ids, weights, sems
):
    copies = [
        pltpu.make_async_copy(ids_ref, ids, sems.at[0]),
        pltpu.make_async_copy(weights_ref, weights, sems.at[1]),
        pltpu.make_async_copy(tokens_ref, held, sems.at[2]),
    ]
    for copy in copies:
        copy.start()
    copies[0].wait()
    copies[1].wait()
    slot_tables(ids, weights, onehot_ref, mix_ref, flight, capacity, orders)
    copies[2].wait()


def pick_kernel(onehot_ref, held_ref, out_ref):
    owners, cores, rows, block = out_ref.shape
    for core in range(cores):
        part = held_ref[:, core * block : (core + 1) * block]
        picked = jnp.dot(onehot_ref[...], part, preferred_element_type=F32).astype(BF16)
        out_ref[:, core] = picked.reshape(owners, rows, block)


def dispatch(ids_t, weights_t, tokens, flight, capacity, shape, orders):
    hbm = pl.BlockSpec(memory_space=pltpu.HBM)
    vmem = pl.BlockSpec(memory_space=pltpu.VMEM)
    slots, tok = flight * capacity, tokens.shape[0]
    held, onehot, mix = pl.pallas_call(
        lambda *refs: read_kernel(flight, capacity, orders, *refs),
        in_specs=[hbm, hbm, hbm],
        out_specs=[vmem, vmem, vmem],
        out_shape=[
            jax.ShapeDtypeStruct(tokens.shape, BF16),
            jax.ShapeDtypeStruct((slots, tok), BF16),
            jax.ShapeDtypeStruct((tok, MIX_PARTS * slots), BF16),
        ],
        scratch_shapes=[
            pltpu.VMEM(ids_t.shape, jnp.int32),
            pltpu.VMEM(weights_t.shape, F32),
            pltpu.SemaphoreType.DMA((3,)),
        ],
        cost_estimate=pl.CostEstimate(flops=0, bytes_accessed=0, transcendentals=0),
        compiler_params=pltpu.CompilerParams(vmem_limit_bytes=16 * 2**20),
    )(*(pltpu.with_memory_space_constraint(a, pltpu.HBM) for a in (ids_t, weights_t, tokens)))
    outgoing = pl.pallas_call(
        pick_kernel,
        in_specs=[vmem, vmem],
        out_specs=vmem,
        out_shape=jax.ShapeDtypeStruct(shape, BF16),
        cost_estimate=pl.CostEstimate(flops=10**11, bytes_accessed=10**8, transcendentals=0),
        compiler_params=pltpu.CompilerParams(vmem_limit_bytes=16 * 2**20),
    )(onehot, held)
    return outgoing, mix


def combine_kernel(mix_ref, rows_ref, out_ref, held, sems):
    copies = []
    for i, at in enumerate(column_blocks(held.shape[1], COMBINE_BLOCKS)):
        rows = jnp.concatenate([rows_ref[:, at]] * MIX_PARTS, axis=0)
        held[:, at] = jnp.dot(mix_ref[...], rows, preferred_element_type=F32).astype(BF16)
        copies.append(pltpu.make_async_copy(held.at[:, at], out_ref.at[:, at], sems.at[i]))
        copies[-1].start()
    for copy in copies:
        copy.wait()


def combine(mix, rows):
    tok, width = mix.shape[0], rows.shape[1]
    vmem = pl.BlockSpec(memory_space=pltpu.VMEM)
    return pl.pallas_call(
        combine_kernel,
        in_specs=[vmem, vmem],
        out_specs=pl.BlockSpec(memory_space=pltpu.HBM),
        out_shape=jax.ShapeDtypeStruct((tok, width), BF16),
        scratch_shapes=[
            pltpu.VMEM((tok, width), BF16),
            pltpu.SemaphoreType.DMA((COMBINE_BLOCKS,)),
        ],
        compiler_params=pltpu.CompilerParams(vmem_limit_bytes=16 * 2**20),
    )(mix, rows)


def whole_call(kernel, out, *arrays):
    return pl.pallas_call(
        kernel,
        in_specs=[pl.BlockSpec(memory_space=pltpu.VMEM)] * len(arrays),
        out_specs=jax.tree.map(lambda _: pl.BlockSpec(memory_space=pltpu.VMEM), out),
        out_shape=out,
        cost_estimate=pl.CostEstimate(flops=2**29, bytes_accessed=0, transcendentals=0),
        compiler_params=pltpu.CompilerParams(vmem_limit_bytes=16 * 2**20),
    )(*arrays)


def up_kernel(x_ref, w_ref, out_ref):
    owners, cores, rows, block = x_ref.shape
    me = lax.axis_index("loop")
    total = None
    for source in range(cores):
        x = x_ref[:, source].reshape(owners * rows, block)
        at = pl.ds(pl.multiple_of((source * cores + me) * block, block), block)
        term = jnp.dot(x, w_ref[0, at, :], preferred_element_type=F32)
        total = term if total is None else total + term
    out_ref[...] = total


def up_first_kernel(x_ref, w_ref, up_ref, down_ref, out_ref):
    up_kernel(x_ref, w_ref, out_ref)


def down_dot(back, part_ref, other_ref, w_ref, core):
    units = part_ref.shape[1]
    sums = part_ref[...] + other_ref[...]
    if back is not None:
        sums = reorder(sums, back, sums.shape[0] // len(back))
    hidden = silu(sums).astype(BF16)
    at = pl.ds(pl.multiple_of(core * units, units), units)
    return jnp.dot(hidden, w_ref[0, at, :], preferred_element_type=F32)


def down_mine_kernel(back, part_ref, other_ref, w_ref, out_ref):
    out_ref[...] = down_dot(back, part_ref, other_ref, w_ref, lax.axis_index("loop"))


def down_theirs_kernel(back, half_ref, part_ref, other_ref, w_ref, out_ref):
    rest = down_dot(back, part_ref, other_ref, w_ref, 1 - lax.axis_index("loop"))
    out_ref[...] = (half_ref[...] + rest).astype(BF16)


def plain_up_kernel(x_ref, w_ref, out_ref):
    out_ref[...] = silu(jnp.dot(x_ref[...], w_ref[0], preferred_element_type=F32)).astype(BF16)


def plain_down_kernel(x_ref, w_ref, out_ref):
    out_ref[...] = jnp.dot(x_ref[...], w_ref[0], preferred_element_type=F32).astype(BF16)


def silu(v):
    return v / (1.0 + jnp.exp(-v))


def on_device(tokens, expert_ids, route_weights, up_proj, down_proj):
    tok_rows, width = tokens.shape
    capacity = tok_rows // 16
    owners = lax.axis_size("expert")
    loops = lax.axis_size("loop")
    per_owner = up_proj.shape[0]
    flight = owners * per_owner
    slots = flight * capacity
    ids_t, weights_t = expert_ids.T, route_weights.T

    orders = back = pairs = singles = None
    if loops == 2 and owners == len(DISPATCH_ORDER) and per_owner == 1:
        orders = (DISPATCH_ORDER, RETURN_ORDER)
        back = [DISPATCH_ORDER.index(owner) for owner in RETURN_ORDER]
        pairs = [[owner * 2 + core for owner in DISPATCH_ORDER for core in range(2)]]
        singles = [RETURN_ORDER]

    if loops == 2:
        block = width // 2
        swap = [(0, 1), (1, 0)]
        up_theirs = lax.ppermute(up_proj, "loop", swap)
        outgoing, mix = dispatch(
            ids_t, weights_t, tokens, flight, capacity, (owners, 2, per_owner * capacity, block), orders
        )
        arrived = lax.all_to_all(
            outgoing.reshape(owners * 2, per_owner * capacity, block),
            ("expert", "loop"),
            split_axis=0,
            concat_axis=0,
            axis_index_groups=pairs,
            tiled=True,
        ).reshape(outgoing.shape)
        units = up_proj.shape[2]
        sums = jax.ShapeDtypeStruct((slots, units), F32)
        part_theirs = whole_call(up_first_kernel, sums, arrived, up_theirs, up_proj, down_proj)
        for_mine = lax.ppermute(part_theirs, "loop", swap)
        part_mine = whole_call(up_kernel, sums, arrived, up_proj)
        for_theirs = lax.ppermute(part_mine, "loop", swap)
        half = whole_call(
            lambda *refs: down_mine_kernel(back, *refs),
            jax.ShapeDtypeStruct((slots, width), F32),
            part_mine,
            for_mine,
            down_proj,
        )
        out_rows = whole_call(
            lambda *refs: down_theirs_kernel(back, *refs),
            jax.ShapeDtypeStruct((slots, width), BF16),
            half,
            part_theirs,
            for_theirs,
            down_proj,
        )
    else:
        outgoing, mix = dispatch(
            ids_t, weights_t, tokens, flight, capacity, (owners, 1, per_owner * capacity, width), None
        )
        arrived = lax.all_to_all(
            outgoing.reshape(owners, per_owner * capacity, width),
            "expert",
            split_axis=0,
            concat_axis=0,
            tiled=True,
        ).reshape(slots, width)
        full = lax.all_gather(arrived, "loop", axis=1, tiled=True)
        hidden = whole_call(
            plain_up_kernel, jax.ShapeDtypeStruct((slots, up_proj.shape[2]), BF16), full, up_proj
        )
        hidden = lax.all_gather(hidden, "loop", axis=1, tiled=True)
        out_rows = whole_call(
            plain_down_kernel, jax.ShapeDtypeStruct((slots, width), BF16), hidden, down_proj
        )

    returned = lax.all_to_all(
        out_rows.reshape(owners, per_owner * capacity, width),
        "expert",
        split_axis=0,
        concat_axis=0,
        axis_index_groups=singles,
        tiled=True,
    ).reshape(slots, width)
    return combine(mix, returned)


def solution(mesh):
    return jax.shard_map(
        on_device,
        mesh=mesh,
        in_specs=(
            P("expert", "loop"),
            P("expert", None),
            P("expert", None),
            P("expert", None, "loop"),
            P("expert", None, "loop"),
        ),
        out_specs=P("expert", "loop"),
        check_vma=False,
    )
```

```python
import jax
import jax.numpy as jnp
from jax import lax
from jax.experimental import pallas as pl
from jax.experimental.pallas import tpu as pltpu
from jax.sharding import PartitionSpec as P

BF16, F32 = jnp.bfloat16, jnp.float32
COMBINE_BLOCKS, MIX_PARTS = 7, 2
DISPATCH_ORDER = [11, 15, 10, 14, 3, 7, 2, 6, 9, 13, 8, 12, 1, 5, 0, 4]
RETURN_ORDER = [11, 3, 10, 2, 9, 1, 8, 0, 15, 7, 14, 6, 13, 5, 12, 4]


def reorder(rows, order, size):
    return jnp.concatenate([rows[i * size : (i + 1) * size] for i in order], axis=0)


def slot_tables(ids_ref, weights_ref, onehot_ref, mix_ref, flight, capacity, orders):
    top, tok = ids_ref.shape
    experts = lax.broadcasted_iota(jnp.int32, (flight, tok), 0)
    chosen = jnp.zeros((flight, tok), F32)
    weight = jnp.zeros((flight, tok), F32)
    for k in range(top):
        names = ids_ref[k : k + 1, :] == experts
        chosen = jnp.where(names, 1.0, chosen)
        weight = jnp.where(names, weights_ref[k : k + 1, :], weight)
    before = lax.broadcasted_iota(jnp.int32, (tok, tok), 0) < lax.broadcasted_iota(
        jnp.int32, (tok, tok), 1
    )
    rank = jnp.dot(
        chosen.astype(BF16), jnp.where(before, 1.0, 0.0).astype(BF16), preferred_element_type=F32
    )
    rank = jnp.where(chosen > 0.5, rank, -1.0)
    places = lax.broadcasted_iota(jnp.int32, (flight, capacity, tok), 1).astype(F32)
    picked = rank[:, None, :] == places
    onehot = jnp.where(picked, 1.0, 0.0).reshape(flight * capacity, tok)
    mix = jnp.where(picked, weight[:, None, :], 0.0).reshape(flight * capacity, tok)
    if orders is not None:
        onehot = reorder(onehot, orders[0], capacity)
        mix = reorder(mix, orders[1], capacity)
    onehot_ref[...] = onehot.astype(BF16)
    mix = mix.T
    slots = flight * capacity
    for i in range(MIX_PARTS):
        part = mix.astype(BF16)
        mix_ref[:, i * slots : (i + 1) * slots] = part
        mix = mix - part.astype(F32)


def column_blocks(width, count):
    block = width // count
    return [slice(i * block, (i + 1) * block) for i in range(count)]


def read_kernel(
    flight, capacity, orders, ids_ref, weights_ref, tokens_ref, held, onehot_ref, mix_ref, ids, weights, sems
):
    copies = [
        pltpu.make_async_copy(ids_ref, ids, sems.at[0]),
        pltpu.make_async_copy(weights_ref, weights, sems.at[1]),
        pltpu.make_async_copy(tokens_ref, held, sems.at[2]),
    ]
    for copy in copies:
        copy.start()
    copies[0].wait()
    copies[1].wait()
    slot_tables(ids, weights, onehot_ref, mix_ref, flight, capacity, orders)
    copies[2].wait()


def pick_kernel(onehot_ref, held_ref, out_ref):
    cores, owners, rows, block = out_ref.shape
    for core in range(cores):
        part = held_ref[:, core * block : (core + 1) * block]
        picked = jnp.dot(onehot_ref[...], part, preferred_element_type=F32).astype(BF16)
        out_ref[core] = picked.reshape(owners, rows, block)


def dispatch(ids_t, weights_t, tokens, flight, capacity, shape, orders):
    hbm = pl.BlockSpec(memory_space=pltpu.HBM)
    vmem = pl.BlockSpec(memory_space=pltpu.VMEM)
    slots, tok = flight * capacity, tokens.shape[0]
    held, onehot, mix = pl.pallas_call(
        lambda *refs: read_kernel(flight, capacity, orders, *refs),
        in_specs=[hbm, hbm, hbm],
        out_specs=[vmem, vmem, vmem],
        out_shape=[
            jax.ShapeDtypeStruct(tokens.shape, BF16),
            jax.ShapeDtypeStruct((slots, tok), BF16),
            jax.ShapeDtypeStruct((tok, MIX_PARTS * slots), BF16),
        ],
        scratch_shapes=[
            pltpu.VMEM(ids_t.shape, jnp.int32),
            pltpu.VMEM(weights_t.shape, F32),
            pltpu.SemaphoreType.DMA((3,)),
        ],
        cost_estimate=pl.CostEstimate(flops=0, bytes_accessed=0, transcendentals=0),
        compiler_params=pltpu.CompilerParams(vmem_limit_bytes=16 * 2**20),
    )(*(pltpu.with_memory_space_constraint(a, pltpu.HBM) for a in (ids_t, weights_t, tokens)))
    outgoing = pl.pallas_call(
        pick_kernel,
        in_specs=[vmem, vmem],
        out_specs=vmem,
        out_shape=jax.ShapeDtypeStruct(shape, BF16),
        cost_estimate=pl.CostEstimate(flops=10**11, bytes_accessed=10**8, transcendentals=0),
        compiler_params=pltpu.CompilerParams(vmem_limit_bytes=16 * 2**20),
    )(onehot, held)
    return outgoing, mix


def combine_kernel(mix_ref, rows_ref, out_ref, held, sems):
    copies = []
    for i, at in enumerate(column_blocks(held.shape[1], COMBINE_BLOCKS)):
        rows = jnp.concatenate([rows_ref[:, at]] * MIX_PARTS, axis=0)
        held[:, at] = jnp.dot(mix_ref[...], rows, preferred_element_type=F32).astype(BF16)
        copies.append(pltpu.make_async_copy(held.at[:, at], out_ref.at[:, at], sems.at[i]))
        copies[-1].start()
    for copy in copies:
        copy.wait()


def combine(mix, rows):
    tok, width = mix.shape[0], rows.shape[1]
    vmem = pl.BlockSpec(memory_space=pltpu.VMEM)
    return pl.pallas_call(
        combine_kernel,
        in_specs=[vmem, vmem],
        out_specs=pl.BlockSpec(memory_space=pltpu.HBM),
        out_shape=jax.ShapeDtypeStruct((tok, width), BF16),
        scratch_shapes=[
            pltpu.VMEM((tok, width), BF16),
            pltpu.SemaphoreType.DMA((COMBINE_BLOCKS,)),
        ],
        compiler_params=pltpu.CompilerParams(vmem_limit_bytes=16 * 2**20),
    )(mix, rows)


def whole_call(kernel, out, *arrays):
    return pl.pallas_call(
        kernel,
        in_specs=[pl.BlockSpec(memory_space=pltpu.VMEM)] * len(arrays),
        out_specs=jax.tree.map(lambda _: pl.BlockSpec(memory_space=pltpu.VMEM), out),
        out_shape=out,
        cost_estimate=pl.CostEstimate(flops=2**29, bytes_accessed=0, transcendentals=0),
        compiler_params=pltpu.CompilerParams(vmem_limit_bytes=16 * 2**20),
    )(*arrays)


def up_kernel(x_ref, w_ref, out_ref):
    cores, owners, rows, block = x_ref.shape
    me = lax.axis_index("loop")
    total = None
    for source in range(cores):
        x = x_ref[source].reshape(owners * rows, block)
        at = pl.ds(pl.multiple_of((source * cores + me) * block, block), block)
        term = jnp.dot(x, w_ref[0, at, :], preferred_element_type=F32)
        total = term if total is None else total + term
    out_ref[...] = total


def up_first_kernel(x_ref, w_ref, up_ref, down_ref, out_ref):
    up_kernel(x_ref, w_ref, out_ref)


def down_dot(back, part_ref, other_ref, w_ref, core):
    units = part_ref.shape[1]
    sums = part_ref[...] + other_ref[...]
    if back is not None:
        sums = reorder(sums, back, sums.shape[0] // len(back))
    hidden = silu(sums).astype(BF16)
    at = pl.ds(pl.multiple_of(core * units, units), units)
    return jnp.dot(hidden, w_ref[0, at, :], preferred_element_type=F32)


def down_mine_kernel(back, part_ref, other_ref, w_ref, out_ref):
    out_ref[...] = down_dot(back, part_ref, other_ref, w_ref, lax.axis_index("loop"))


def down_theirs_kernel(back, half_ref, part_ref, other_ref, w_ref, out_ref):
    rest = down_dot(back, part_ref, other_ref, w_ref, 1 - lax.axis_index("loop"))
    out_ref[...] = (half_ref[...] + rest).astype(BF16)


def plain_up_kernel(x_ref, w_ref, out_ref):
    out_ref[...] = silu(jnp.dot(x_ref[...], w_ref[0], preferred_element_type=F32)).astype(BF16)


def plain_down_kernel(x_ref, w_ref, out_ref):
    out_ref[...] = jnp.dot(x_ref[...], w_ref[0], preferred_element_type=F32).astype(BF16)


def silu(v):
    return v / (1.0 + jnp.exp(-v))


def on_device(tokens, expert_ids, route_weights, up_proj, down_proj):
    tok_rows, width = tokens.shape
    capacity = tok_rows // 16
    owners = lax.axis_size("expert")
    loops = lax.axis_size("loop")
    per_owner = up_proj.shape[0]
    flight = owners * per_owner
    slots = flight * capacity
    ids_t, weights_t = expert_ids.T, route_weights.T

    orders = back = singles = None
    pairs = [[owner * 2 + core for core in range(2) for owner in range(owners)]]
    if loops == 2 and owners == len(DISPATCH_ORDER) and per_owner == 1:
        orders = (DISPATCH_ORDER, RETURN_ORDER)
        back = [DISPATCH_ORDER.index(owner) for owner in RETURN_ORDER]
        pairs = [[owner * 2 + core for core in range(2) for owner in DISPATCH_ORDER]]
        singles = [RETURN_ORDER]

    if loops == 2:
        block = width // 2
        swap = [(0, 1), (1, 0)]
        up_theirs = lax.ppermute(up_proj, "loop", swap)
        outgoing, mix = dispatch(
            ids_t, weights_t, tokens, flight, capacity, (2, owners, per_owner * capacity, block), orders
        )
        arrived = lax.all_to_all(
            outgoing.reshape(owners * 2, per_owner * capacity, block),
            ("expert", "loop"),
            split_axis=0,
            concat_axis=0,
            axis_index_groups=pairs,
            tiled=True,
        ).reshape(outgoing.shape)
        units = up_proj.shape[2]
        sums = jax.ShapeDtypeStruct((slots, units), F32)
        part_theirs = whole_call(up_first_kernel, sums, arrived, up_theirs, up_proj, down_proj)
        for_mine = lax.ppermute(part_theirs, "loop", swap)
        part_mine = whole_call(up_kernel, sums, arrived, up_proj)
        for_theirs = lax.ppermute(part_mine, "loop", swap)
        half = whole_call(
            lambda *refs: down_mine_kernel(back, *refs),
            jax.ShapeDtypeStruct((slots, width), F32),
            part_mine,
            for_mine,
            down_proj,
        )
        out_rows = whole_call(
            lambda *refs: down_theirs_kernel(back, *refs),
            jax.ShapeDtypeStruct((slots, width), BF16),
            half,
            part_theirs,
            for_theirs,
            down_proj,
        )
    else:
        outgoing, mix = dispatch(
            ids_t, weights_t, tokens, flight, capacity, (1, owners, per_owner * capacity, width), None
        )
        arrived = lax.all_to_all(
            outgoing.reshape(owners, per_owner * capacity, width),
            "expert",
            split_axis=0,
            concat_axis=0,
            tiled=True,
        ).reshape(slots, width)
        full = lax.all_gather(arrived, "loop", axis=1, tiled=True)
        hidden = whole_call(
            plain_up_kernel, jax.ShapeDtypeStruct((slots, up_proj.shape[2]), BF16), full, up_proj
        )
        hidden = lax.all_gather(hidden, "loop", axis=1, tiled=True)
        out_rows = whole_call(
            plain_down_kernel, jax.ShapeDtypeStruct((slots, width), BF16), hidden, down_proj
        )

    returned = lax.all_to_all(
        out_rows.reshape(owners, per_owner * capacity, width),
        "expert",
        split_axis=0,
        concat_axis=0,
        axis_index_groups=singles,
        tiled=True,
    ).reshape(slots, width)
    return combine(mix, returned)


def solution(mesh):
    return jax.shard_map(
        on_device,
        mesh=mesh,
        in_specs=(
            P("expert", "loop"),
            P("expert", None),
            P("expert", None),
            P("expert", None, "loop"),
            P("expert", None, "loop"),
        ),
        out_specs=P("expert", "loop"),
        check_vma=False,
    )
```

```python
import jax
import jax.numpy as jnp
from jax import lax
from jax.experimental import pallas as pl
from jax.experimental.pallas import tpu as pltpu
from jax.sharding import PartitionSpec as P

BF16, F32 = jnp.bfloat16, jnp.float32
COMBINE_BLOCKS, MIX_PARTS = 7, 2
DISPATCH_ORDER = [11, 15, 10, 14, 3, 7, 2, 6, 9, 13, 8, 12, 1, 5, 0, 4]
RETURN_ORDER = [11, 3, 10, 2, 9, 1, 8, 0, 15, 7, 14, 6, 13, 5, 12, 4]


def reorder(rows, order, size):
    return jnp.concatenate([rows[i * size : (i + 1) * size] for i in order], axis=0)


def slot_tables(ids_ref, weights_ref, onehot_ref, mix_ref, flight, capacity, orders):
    top, tok = ids_ref.shape
    experts = lax.broadcasted_iota(jnp.int32, (flight, tok), 0)
    chosen = jnp.zeros((flight, tok), F32)
    weight = jnp.zeros((flight, tok), F32)
    for k in range(top):
        names = ids_ref[k : k + 1, :] == experts
        chosen = jnp.where(names, 1.0, chosen)
        weight = jnp.where(names, weights_ref[k : k + 1, :], weight)
    before = lax.broadcasted_iota(jnp.int32, (tok, tok), 0) < lax.broadcasted_iota(
        jnp.int32, (tok, tok), 1
    )
    rank = jnp.dot(
        chosen.astype(BF16), jnp.where(before, 1.0, 0.0).astype(BF16), preferred_element_type=F32
    )
    rank = jnp.where(chosen > 0.5, rank, -1.0)
    places = lax.broadcasted_iota(jnp.int32, (flight, capacity, tok), 1).astype(F32)
    picked = rank[:, None, :] == places
    onehot = jnp.where(picked, 1.0, 0.0).reshape(flight * capacity, tok)
    mix = jnp.where(picked, weight[:, None, :], 0.0).reshape(flight * capacity, tok)
    if orders is not None:
        onehot = reorder(onehot, orders[0], capacity)
        mix = reorder(mix, orders[1], capacity)
    onehot_ref[...] = onehot.astype(BF16)
    mix = mix.T
    slots = flight * capacity
    for i in range(MIX_PARTS):
        part = mix.astype(BF16)
        mix_ref[:, i * slots : (i + 1) * slots] = part
        mix = mix - part.astype(F32)


def column_blocks(width, count):
    block = width // count
    return [slice(i * block, (i + 1) * block) for i in range(count)]


def read_kernel(flight, capacity, orders, ids_ref, weights_ref, onehot_ref, mix_ref, ids, weights, sems):
    copies = [
        pltpu.make_async_copy(ids_ref, ids, sems.at[0]),
        pltpu.make_async_copy(weights_ref, weights, sems.at[1]),
    ]
    for copy in copies:
        copy.start()
    for copy in copies:
        copy.wait()
    slot_tables(ids, weights, onehot_ref, mix_ref, flight, capacity, orders)


def pick_kernel(onehot_ref, held_ref, out_ref):
    cores, owners, rows, block = out_ref.shape
    for core in range(cores):
        part = held_ref[:, core * block : (core + 1) * block]
        picked = jnp.dot(onehot_ref[...], part, preferred_element_type=F32).astype(BF16)
        out_ref[core] = picked.reshape(owners, rows, block)


def dispatch(ids_t, weights_t, tokens, flight, capacity, shape, orders):
    hbm = pl.BlockSpec(memory_space=pltpu.HBM)
    vmem = pl.BlockSpec(memory_space=pltpu.VMEM)
    slots, tok = flight * capacity, tokens.shape[0]
    onehot, mix = pl.pallas_call(
        lambda *refs: read_kernel(flight, capacity, orders, *refs),
        in_specs=[hbm, hbm],
        out_specs=[vmem, vmem],
        out_shape=[
            jax.ShapeDtypeStruct((slots, tok), BF16),
            jax.ShapeDtypeStruct((tok, MIX_PARTS * slots), BF16),
        ],
        scratch_shapes=[
            pltpu.VMEM(ids_t.shape, jnp.int32),
            pltpu.VMEM(weights_t.shape, F32),
            pltpu.SemaphoreType.DMA((2,)),
        ],
        cost_estimate=pl.CostEstimate(flops=2**31, bytes_accessed=0, transcendentals=0),
        compiler_params=pltpu.CompilerParams(vmem_limit_bytes=16 * 2**20),
    )(*(pltpu.with_memory_space_constraint(a, pltpu.HBM) for a in (ids_t, weights_t)))
    outgoing = pl.pallas_call(
        pick_kernel,
        in_specs=[vmem, vmem],
        out_specs=vmem,
        out_shape=jax.ShapeDtypeStruct(shape, BF16),
        cost_estimate=pl.CostEstimate(flops=10**11, bytes_accessed=10**8, transcendentals=0),
        compiler_params=pltpu.CompilerParams(vmem_limit_bytes=16 * 2**20),
    )(onehot, tokens)
    return outgoing, mix


def combine_kernel(mix_ref, rows_ref, out_ref, held, sems):
    copies = []
    for i, at in enumerate(column_blocks(held.shape[1], COMBINE_BLOCKS)):
        rows = jnp.concatenate([rows_ref[:, at]] * MIX_PARTS, axis=0)
        held[:, at] = jnp.dot(mix_ref[...], rows, preferred_element_type=F32).astype(BF16)
        copies.append(pltpu.make_async_copy(held.at[:, at], out_ref.at[:, at], sems.at[i]))
        copies[-1].start()
    for copy in copies:
        copy.wait()


def combine(mix, rows):
    tok, width = mix.shape[0], rows.shape[1]
    vmem = pl.BlockSpec(memory_space=pltpu.VMEM)
    return pl.pallas_call(
        combine_kernel,
        in_specs=[vmem, vmem],
        out_specs=pl.BlockSpec(memory_space=pltpu.HBM),
        out_shape=jax.ShapeDtypeStruct((tok, width), BF16),
        scratch_shapes=[
            pltpu.VMEM((tok, width), BF16),
            pltpu.SemaphoreType.DMA((COMBINE_BLOCKS,)),
        ],
        compiler_params=pltpu.CompilerParams(vmem_limit_bytes=16 * 2**20),
    )(mix, rows)


def whole_call(kernel, out, *arrays):
    return pl.pallas_call(
        kernel,
        in_specs=[pl.BlockSpec(memory_space=pltpu.VMEM)] * len(arrays),
        out_specs=jax.tree.map(lambda _: pl.BlockSpec(memory_space=pltpu.VMEM), out),
        out_shape=out,
        cost_estimate=pl.CostEstimate(flops=2**29, bytes_accessed=0, transcendentals=0),
        compiler_params=pltpu.CompilerParams(vmem_limit_bytes=16 * 2**20),
    )(*arrays)


def up_kernel(x_ref, w_ref, out_ref):
    cores, owners, rows, block = x_ref.shape
    me = lax.axis_index("loop")
    total = None
    for source in range(cores):
        x = x_ref[source].reshape(owners * rows, block)
        at = pl.ds(pl.multiple_of((source * cores + me) * block, block), block)
        term = jnp.dot(x, w_ref[0, at, :], preferred_element_type=F32)
        total = term if total is None else total + term
    out_ref[...] = total


def up_first_kernel(x_ref, w_ref, up_ref, down_ref, out_ref):
    up_kernel(x_ref, w_ref, out_ref)


def down_dot(back, part_ref, other_ref, w_ref, core):
    units = part_ref.shape[1]
    sums = part_ref[...] + other_ref[...]
    if back is not None:
        sums = reorder(sums, back, sums.shape[0] // len(back))
    hidden = silu(sums).astype(BF16)
    at = pl.ds(pl.multiple_of(core * units, units), units)
    return jnp.dot(hidden, w_ref[0, at, :], preferred_element_type=F32)


def down_mine_kernel(back, part_ref, other_ref, w_ref, out_ref):
    out_ref[...] = down_dot(back, part_ref, other_ref, w_ref, lax.axis_index("loop"))


def down_theirs_kernel(back, half_ref, part_ref, other_ref, w_ref, out_ref):
    rest = down_dot(back, part_ref, other_ref, w_ref, 1 - lax.axis_index("loop"))
    out_ref[...] = (half_ref[...] + rest).astype(BF16)


def plain_up_kernel(x_ref, w_ref, out_ref):
    out_ref[...] = silu(jnp.dot(x_ref[...], w_ref[0], preferred_element_type=F32)).astype(BF16)


def plain_down_kernel(x_ref, w_ref, out_ref):
    out_ref[...] = jnp.dot(x_ref[...], w_ref[0], preferred_element_type=F32).astype(BF16)


def silu(v):
    return v / (1.0 + jnp.exp(-v))


def on_device(tokens, expert_ids, route_weights, up_proj, down_proj):
    tok_rows, width = tokens.shape
    capacity = tok_rows // 16
    owners = lax.axis_size("expert")
    loops = lax.axis_size("loop")
    per_owner = up_proj.shape[0]
    flight = owners * per_owner
    slots = flight * capacity
    ids_t, weights_t = expert_ids.T, route_weights.T

    orders = back = singles = None
    pairs = [[owner * 2 + core for core in range(2) for owner in range(owners)]]
    if loops == 2 and owners == len(DISPATCH_ORDER) and per_owner == 1:
        orders = (DISPATCH_ORDER, RETURN_ORDER)
        back = [DISPATCH_ORDER.index(owner) for owner in RETURN_ORDER]
        pairs = [[owner * 2 + core for core in range(2) for owner in DISPATCH_ORDER]]
        singles = [RETURN_ORDER]

    if loops == 2:
        block = width // 2
        swap = [(0, 1), (1, 0)]
        up_theirs = lax.ppermute(up_proj, "loop", swap)
        outgoing, mix = dispatch(
            ids_t, weights_t, tokens, flight, capacity, (2, owners, per_owner * capacity, block), orders
        )
        arrived = lax.all_to_all(
            outgoing.reshape(owners * 2, per_owner * capacity, block),
            ("expert", "loop"),
            split_axis=0,
            concat_axis=0,
            axis_index_groups=pairs,
            tiled=True,
        ).reshape(outgoing.shape)
        units = up_proj.shape[2]
        sums = jax.ShapeDtypeStruct((slots, units), F32)
        part_theirs = whole_call(up_first_kernel, sums, arrived, up_theirs, up_proj, down_proj)
        for_mine = lax.ppermute(part_theirs, "loop", swap)
        part_mine = whole_call(up_kernel, sums, arrived, up_proj)
        for_theirs = lax.ppermute(part_mine, "loop", swap)
        half = whole_call(
            lambda *refs: down_mine_kernel(back, *refs),
            jax.ShapeDtypeStruct((slots, width), F32),
            part_mine,
            for_mine,
            down_proj,
        )
        out_rows = whole_call(
            lambda *refs: down_theirs_kernel(back, *refs),
            jax.ShapeDtypeStruct((slots, width), BF16),
            half,
            part_theirs,
            for_theirs,
            down_proj,
        )
    else:
        outgoing, mix = dispatch(
            ids_t, weights_t, tokens, flight, capacity, (1, owners, per_owner * capacity, width), None
        )
        arrived = lax.all_to_all(
            outgoing.reshape(owners, per_owner * capacity, width),
            "expert",
            split_axis=0,
            concat_axis=0,
            tiled=True,
        ).reshape(slots, width)
        full = lax.all_gather(arrived, "loop", axis=1, tiled=True)
        hidden = whole_call(
            plain_up_kernel, jax.ShapeDtypeStruct((slots, up_proj.shape[2]), BF16), full, up_proj
        )
        hidden = lax.all_gather(hidden, "loop", axis=1, tiled=True)
        out_rows = whole_call(
            plain_down_kernel, jax.ShapeDtypeStruct((slots, width), BF16), hidden, down_proj
        )

    returned = lax.all_to_all(
        out_rows.reshape(owners, per_owner * capacity, width),
        "expert",
        split_axis=0,
        concat_axis=0,
        axis_index_groups=singles,
        tiled=True,
    ).reshape(slots, width)
    return combine(mix, returned)


def solution(mesh):
    return jax.shard_map(
        on_device,
        mesh=mesh,
        in_specs=(
            P("expert", "loop"),
            P("expert", None),
            P("expert", None),
            P("expert", None, "loop"),
            P("expert", None, "loop"),
        ),
        out_specs=P("expert", "loop"),
        check_vma=False,
    )
```

```python
import jax
import jax.numpy as jnp
from jax import lax
from jax.experimental import pallas as pl
from jax.experimental.pallas import tpu as pltpu
from jax.sharding import PartitionSpec as P

BF16, F32 = jnp.bfloat16, jnp.float32
COMBINE_BLOCKS, MIX_PARTS = 7, 2
DISPATCH_ORDER = [11, 15, 10, 14, 3, 7, 2, 6, 9, 13, 8, 12, 1, 5, 0, 4]
RETURN_ORDER = [11, 3, 10, 13, 9, 1, 8, 0, 15, 7, 14, 6, 2, 5, 12, 4]


def reorder(rows, order, size):
    return jnp.concatenate([rows[i * size : (i + 1) * size] for i in order], axis=0)


def slot_tables(ids_ref, weights_ref, onehot_ref, mix_ref, flight, capacity, orders):
    top, tok = ids_ref.shape
    experts = lax.broadcasted_iota(jnp.int32, (flight, tok), 0)
    chosen = jnp.zeros((flight, tok), F32)
    weight = jnp.zeros((flight, tok), F32)
    for k in range(top):
        names = ids_ref[k : k + 1, :] == experts
        chosen = jnp.where(names, 1.0, chosen)
        weight = jnp.where(names, weights_ref[k : k + 1, :], weight)
    before = lax.broadcasted_iota(jnp.int32, (tok, tok), 0) < lax.broadcasted_iota(
        jnp.int32, (tok, tok), 1
    )
    rank = jnp.dot(
        chosen.astype(BF16), jnp.where(before, 1.0, 0.0).astype(BF16), preferred_element_type=F32
    )
    rank = jnp.where(chosen > 0.5, rank, -1.0)
    places = lax.broadcasted_iota(jnp.int32, (flight, capacity, tok), 1).astype(F32)
    picked = rank[:, None, :] == places
    onehot = jnp.where(picked, 1.0, 0.0).reshape(flight * capacity, tok)
    mix = jnp.where(picked, weight[:, None, :], 0.0).reshape(flight * capacity, tok)
    if orders is not None:
        onehot = reorder(onehot, orders[0], capacity)
        mix = reorder(mix, orders[1], capacity)
    onehot_ref[...] = onehot.astype(BF16)
    mix = mix.T
    slots = flight * capacity
    for i in range(MIX_PARTS):
        part = mix.astype(BF16)
        mix_ref[:, i * slots : (i + 1) * slots] = part
        mix = mix - part.astype(F32)


def column_blocks(width, count):
    block = width // count
    return [slice(i * block, (i + 1) * block) for i in range(count)]


def read_kernel(flight, capacity, orders, ids_ref, weights_ref, onehot_ref, mix_ref, ids, weights, sems):
    copies = [
        pltpu.make_async_copy(ids_ref, ids, sems.at[0]),
        pltpu.make_async_copy(weights_ref, weights, sems.at[1]),
    ]
    for copy in copies:
        copy.start()
    for copy in copies:
        copy.wait()
    slot_tables(ids, weights, onehot_ref, mix_ref, flight, capacity, orders)


def pick_kernel(onehot_ref, held_ref, out_ref):
    cores, owners, rows, block = out_ref.shape
    for core in range(cores):
        part = held_ref[:, core * block : (core + 1) * block]
        picked = jnp.dot(onehot_ref[...], part, preferred_element_type=F32).astype(BF16)
        out_ref[core] = picked.reshape(owners, rows, block)


def dispatch(ids_t, weights_t, tokens, flight, capacity, shape, orders):
    hbm = pl.BlockSpec(memory_space=pltpu.HBM)
    vmem = pl.BlockSpec(memory_space=pltpu.VMEM)
    slots, tok = flight * capacity, tokens.shape[0]
    onehot, mix = pl.pallas_call(
        lambda *refs: read_kernel(flight, capacity, orders, *refs),
        in_specs=[hbm, hbm],
        out_specs=[vmem, vmem],
        out_shape=[
            jax.ShapeDtypeStruct((slots, tok), BF16),
            jax.ShapeDtypeStruct((tok, MIX_PARTS * slots), BF16),
        ],
        scratch_shapes=[
            pltpu.VMEM(ids_t.shape, jnp.int32),
            pltpu.VMEM(weights_t.shape, F32),
            pltpu.SemaphoreType.DMA((2,)),
        ],
        cost_estimate=pl.CostEstimate(flops=2**31, bytes_accessed=0, transcendentals=0),
        compiler_params=pltpu.CompilerParams(vmem_limit_bytes=16 * 2**20),
    )(*(pltpu.with_memory_space_constraint(a, pltpu.HBM) for a in (ids_t, weights_t)))
    outgoing = pl.pallas_call(
        pick_kernel,
        in_specs=[vmem, vmem],
        out_specs=vmem,
        out_shape=jax.ShapeDtypeStruct(shape, BF16),
        cost_estimate=pl.CostEstimate(flops=10**11, bytes_accessed=10**8, transcendentals=0),
        compiler_params=pltpu.CompilerParams(vmem_limit_bytes=16 * 2**20),
    )(onehot, tokens)
    return outgoing, mix


def combine_kernel(mix_ref, rows_ref, out_ref, held, sems):
    copies = []
    for i, at in enumerate(column_blocks(held.shape[1], COMBINE_BLOCKS)):
        rows = jnp.concatenate([rows_ref[:, at]] * MIX_PARTS, axis=0)
        held[:, at] = jnp.dot(mix_ref[...], rows, preferred_element_type=F32).astype(BF16)
        copies.append(pltpu.make_async_copy(held.at[:, at], out_ref.at[:, at], sems.at[i]))
        copies[-1].start()
    for copy in copies:
        copy.wait()


def combine(mix, rows):
    tok, width = mix.shape[0], rows.shape[1]
    vmem = pl.BlockSpec(memory_space=pltpu.VMEM)
    return pl.pallas_call(
        combine_kernel,
        in_specs=[vmem, vmem],
        out_specs=pl.BlockSpec(memory_space=pltpu.HBM),
        out_shape=jax.ShapeDtypeStruct((tok, width), BF16),
        scratch_shapes=[
            pltpu.VMEM((tok, width), BF16),
            pltpu.SemaphoreType.DMA((COMBINE_BLOCKS,)),
        ],
        compiler_params=pltpu.CompilerParams(vmem_limit_bytes=16 * 2**20),
    )(mix, rows)


def whole_call(kernel, out, *arrays):
    return pl.pallas_call(
        kernel,
        in_specs=[pl.BlockSpec(memory_space=pltpu.VMEM)] * len(arrays),
        out_specs=jax.tree.map(lambda _: pl.BlockSpec(memory_space=pltpu.VMEM), out),
        out_shape=out,
        cost_estimate=pl.CostEstimate(flops=2**29, bytes_accessed=0, transcendentals=0),
        compiler_params=pltpu.CompilerParams(vmem_limit_bytes=16 * 2**20),
    )(*arrays)


def up_kernel(x_ref, w_ref, out_ref):
    cores, owners, rows, block = x_ref.shape
    me = lax.axis_index("loop")
    total = None
    for source in range(cores):
        x = x_ref[source].reshape(owners * rows, block)
        at = pl.ds(pl.multiple_of((source * cores + me) * block, block), block)
        term = jnp.dot(x, w_ref[0, at, :], preferred_element_type=F32)
        total = term if total is None else total + term
    out_ref[...] = total


def up_first_kernel(x_ref, w_ref, up_ref, down_ref, out_ref):
    up_kernel(x_ref, w_ref, out_ref)


def down_dot(back, part_ref, other_ref, w_ref, core):
    units = part_ref.shape[1]
    sums = part_ref[...] + other_ref[...]
    if back is not None:
        sums = reorder(sums, back, sums.shape[0] // len(back))
    hidden = silu(sums).astype(BF16)
    at = pl.ds(pl.multiple_of(core * units, units), units)
    return jnp.dot(hidden, w_ref[0, at, :], preferred_element_type=F32)


def down_mine_kernel(back, part_ref, other_ref, w_ref, out_ref):
    out_ref[...] = down_dot(back, part_ref, other_ref, w_ref, lax.axis_index("loop"))


def down_theirs_kernel(back, half_ref, part_ref, other_ref, w_ref, out_ref):
    rest = down_dot(back, part_ref, other_ref, w_ref, 1 - lax.axis_index("loop"))
    out_ref[...] = (half_ref[...] + rest).astype(BF16)


def plain_up_kernel(x_ref, w_ref, out_ref):
    out_ref[...] = silu(jnp.dot(x_ref[...], w_ref[0], preferred_element_type=F32)).astype(BF16)


def plain_down_kernel(x_ref, w_ref, out_ref):
    out_ref[...] = jnp.dot(x_ref[...], w_ref[0], preferred_element_type=F32).astype(BF16)


def silu(v):
    return v / (1.0 + jnp.exp(-v))


def on_device(tokens, expert_ids, route_weights, up_proj, down_proj):
    tok_rows, width = tokens.shape
    capacity = tok_rows // 16
    owners = lax.axis_size("expert")
    loops = lax.axis_size("loop")
    per_owner = up_proj.shape[0]
    flight = owners * per_owner
    slots = flight * capacity
    ids_t, weights_t = expert_ids.T, route_weights.T

    orders = back = singles = None
    pairs = [[owner * 2 + core for core in range(2) for owner in range(owners)]]
    if loops == 2 and owners == len(DISPATCH_ORDER) and per_owner == 1:
        orders = (DISPATCH_ORDER, RETURN_ORDER)
        back = [DISPATCH_ORDER.index(owner) for owner in RETURN_ORDER]
        pairs = [[owner * 2 + core for core in range(2) for owner in DISPATCH_ORDER]]
        singles = [RETURN_ORDER]

    if loops == 2:
        block = width // 2
        swap = [(0, 1), (1, 0)]
        up_theirs = lax.ppermute(up_proj, "loop", swap)
        outgoing, mix = dispatch(
            ids_t, weights_t, tokens, flight, capacity, (2, owners, per_owner * capacity, block), orders
        )
        arrived = lax.all_to_all(
            outgoing.reshape(owners * 2, per_owner * capacity, block),
            ("expert", "loop"),
            split_axis=0,
            concat_axis=0,
            axis_index_groups=pairs,
            tiled=True,
        ).reshape(outgoing.shape)
        units = up_proj.shape[2]
        sums = jax.ShapeDtypeStruct((slots, units), F32)
        part_theirs = whole_call(up_first_kernel, sums, arrived, up_theirs, up_proj, down_proj)
        for_mine = lax.ppermute(part_theirs, "loop", swap)
        part_mine = whole_call(up_kernel, sums, arrived, up_proj)
        for_theirs = lax.ppermute(part_mine, "loop", swap)
        half = whole_call(
            lambda *refs: down_mine_kernel(back, *refs),
            jax.ShapeDtypeStruct((slots, width), F32),
            part_mine,
            for_mine,
            down_proj,
        )
        out_rows = whole_call(
            lambda *refs: down_theirs_kernel(back, *refs),
            jax.ShapeDtypeStruct((slots, width), BF16),
            half,
            part_theirs,
            for_theirs,
            down_proj,
        )
    else:
        outgoing, mix = dispatch(
            ids_t, weights_t, tokens, flight, capacity, (1, owners, per_owner * capacity, width), None
        )
        arrived = lax.all_to_all(
            outgoing.reshape(owners, per_owner * capacity, width),
            "expert",
            split_axis=0,
            concat_axis=0,
            tiled=True,
        ).reshape(slots, width)
        full = lax.all_gather(arrived, "loop", axis=1, tiled=True)
        hidden = whole_call(
            plain_up_kernel, jax.ShapeDtypeStruct((slots, up_proj.shape[2]), BF16), full, up_proj
        )
        hidden = lax.all_gather(hidden, "loop", axis=1, tiled=True)
        out_rows = whole_call(
            plain_down_kernel, jax.ShapeDtypeStruct((slots, width), BF16), hidden, down_proj
        )

    returned = lax.all_to_all(
        out_rows.reshape(owners, per_owner * capacity, width),
        "expert",
        split_axis=0,
        concat_axis=0,
        axis_index_groups=singles,
        tiled=True,
    ).reshape(slots, width)
    return combine(mix, returned)


def solution(mesh):
    return jax.shard_map(
        on_device,
        mesh=mesh,
        in_specs=(
            P("expert", "loop"),
            P("expert", None),
            P("expert", None),
            P("expert", None, "loop"),
            P("expert", None, "loop"),
        ),
        out_specs=P("expert", "loop"),
        check_vma=False,
    )
```
